32 devices in a mesh: grp: 4 (over y, x), ctx: 8 (over z, core).
Axes of the slice: x: 2, y: 2, z: 4, core: 2. Of those that a mesh axis runs over, the one named last changes fastest.
Arguments:
- queries: bfloat16 [4096, 2048], P(('grp', 'ctx')), parts along dimension 0, may hold values from -80 to 80
- keys: bfloat16 [4096, 512], P(('grp', 'ctx')), parts along dimension 0, may hold values from -4 to 4
- values: bfloat16 [4096, 512], P(('grp', 'ctx')), parts along dimension 0, may hold values from -6 to 6
- doc_lengths: int32 [32], P('grp'), parts along dimension 0, may hold values from 1 to 256, 1024 in all
- loader_pos: int32 [4096], P(('grp', 'ctx')), parts along dimension 0, may hold values from 0 to 1023, as said below
Outputs:
- attended: bfloat16 [4096, 2048], P(('grp', 'ctx')), parts along dimension 0
The draws below stay inside these ranges and needn't reach their ends.
There are 4 independent parts, one for each index of `grp`. The reference program is written for one: setup_inputs(seed, part) draws one part's arguments, and reference() takes and returns one part's arrays. A program takes and returns all parts, laid end to end along the dimension named above; each array names one. Nothing has to cross between parts.
Inputs may be any that keep to these rules, and one draw needn't show every extreme that they name: loader_pos is a permutation of the packed positions; each block of 128 rows of it holds exactly 16 positions of every block of 128 consecutive packed positions.
All inputs are finite; a program needn't handle non-finite values.
Results may differ from the reference program's by a relative error of at most 0.0033.
Values may be sent and summed in bfloat16 or wider, within the bound.
No kernel may reach another device: no remote copies, remote signals or barrier semaphores. Data moves between devices by JAX's collectives and lax.ppermute only.
A program may use at most 64 MiB of HBM per device.

```python
import math
import jax
import jax.numpy as jnp
import numpy as np
from jax import lax

QUERY_HEADS = 16
KEY_VALUE_HEADS = 4
HEAD_WIDTH = 128
TOK_DEV = 128
PACKED_TOKENS = 1024
LONGEST_DOCUMENT = 256
NDOCS = 8
N_CTX = 8


def loader_table(key):
    base_key = jax.random.fold_in(key, 101)
    first_key, second_key = jax.random.split(base_key)
    shard_count = N_CTX
    shard_rows = TOK_DEV
    cap_rows = shard_rows // shard_count
    block_score = jax.random.randint(first_key, (shard_count, shard_count), 0, 2 ** 20) * shard_count + jnp.arange(shard_count)[None, :]
    blocks = jnp.argsort(block_score, axis=1).astype(jnp.int32)
    slots = jnp.arange(shard_rows, dtype=jnp.int32)
    target = slots // cap_rows
    inner_slot = slots % cap_rows
    source = jnp.arange(shard_count, dtype=jnp.int32)[:, None]
    value_table = target[None, :] * shard_rows + blocks[target[None, :], source] * cap_rows + inner_slot[None, :]
    shuffle_score = jax.random.randint(second_key, (shard_count, shard_rows), 0, 2 ** 20) * shard_rows + slots[None, :]
    shuffle = jnp.argsort(shuffle_score, axis=1)
    return jnp.take_along_axis(value_table, shuffle, axis=1).reshape(-1).astype(jnp.int32)


def packed_keys(key):
    random_jitter = jnp.clip(jax.random.normal(jax.random.fold_in(key, 202), (PACKED_TOKENS, KEY_VALUE_HEADS * HEAD_WIDTH), jnp.float32), -4.0, 4.0)
    return random_jitter


def draw_loader_pos(key, part):
    return loader_table(key)


def draw_keys(key, part):
    return packed_keys(key)[loader_table(key)].astype(jnp.bfloat16)


def draw_queries(key, part):
    base_rows = jnp.clip(jax.random.normal(jax.random.fold_in(key, 303), (PACKED_TOKENS, QUERY_HEADS * HEAD_WIDTH), jnp.float32), -4.0, 4.0)
    return base_rows[loader_table(key)].astype(jnp.bfloat16)


def shard_levels(rng, dims, cuts, smallest, top_value):
    gain = 1.0
    for dim, blocks in cuts:
        draws = jax.random.uniform(jax.random.fold_in(jax.random.fold_in(rng, 6), dim), (blocks,), jnp.float32, smallest / len(cuts), top_value / len(cuts))
        gain = gain * jnp.repeat(jnp.exp(draws), dims[dim] // blocks).reshape((-1,) + (1,) * (len(dims) - 1 - dim))
    return gain


def profile(amount, total, most, skew):
    weights = [(1 << 20) // math.isqrt(standing ** skew) + 1 for standing in range(2, amount + 1)]
    rest, given = total - most - (amount - 1), [1] * (amount - 1)
    while rest > 0:
        movable = [i for i in range(amount - 1) if given[i] < most]
        pool, remaining = sum([weights[i] for i in movable]), rest
        for i in movable:
            more = min(most - given[i], max(1, remaining * weights[i] // pool), rest)
            given[i] = given[i] + more
            rest = rest - more
    return np.array([most] + given)


def uneven_parts(own_key, number_of, total, reach, slope):
    if number_of == 2:
        one = jax.random.randint(own_key, (), max(1, total - reach), min(reach, total - 1) + 1)
        return jnp.stack([one, total - one])
    sizes = jnp.asarray(profile(number_of, total, reach, slope), jnp.int32)
    couples = (number_of - 1) // 2
    giver, taker = sizes[1:1 + 2 * couples:2], sizes[2:2 + 2 * couples:2]
    room = jnp.minimum(giver - 1, reach - taker)
    shifted = jax.random.randint(jax.random.fold_in(own_key, 1), (couples,), 0, 1 << 20) % (room + 1)
    sizes = sizes.at[1:1 + 2 * couples:2].set(giver - shifted).at[2:2 + 2 * couples:2].set(taker + shifted)
    return sizes[jax.random.permutation(jax.random.fold_in(own_key, 2), number_of)]


def bell_draw(stream_key, shape, scale, limit, shards=(), held_as=jnp.bfloat16):
    drawn = jax.random.normal(stream_key, shape, jnp.float32) * scale
    if len(shards) > 0:
        drawn = shard_levels(stream_key, shape, shards, -0.22, 0.18) * drawn
    return jnp.clip(drawn, min=-limit, max=limit).astype(held_as)


def setup_inputs(seed: int = 0, part: int = 0) -> dict:
    key_list = jax.random.split(jax.random.key(seed), 6)
    part_splits = jax.random.split(jax.random.fold_in(key_list[5], part), 6)
    return {
        "queries": draw_queries(jax.random.fold_in(jax.random.fold_in(key_list[5], part), 71), part),
        "keys": draw_keys(jax.random.fold_in(jax.random.fold_in(key_list[5], part), 71), part),
        "values": bell_draw(part_splits[2], (PACKED_TOKENS, KEY_VALUE_HEADS * HEAD_WIDTH), 1.0, 6.0, ((0, 8),)),
        "doc_lengths": uneven_parts(part_splits[3], NDOCS, PACKED_TOKENS, LONGEST_DOCUMENT, 2).astype(jnp.int32),
        "loader_pos": draw_loader_pos(jax.random.fold_in(jax.random.fold_in(key_list[5], part), 71), part),
    }


masked_value = -1e30


def doc_index(positions, ends):
    return jnp.sum((positions[:, None] >= ends[None, :]).astype(jnp.int32), axis=1)


def attend(query_rows, k_win, v_win, q_pos, k_pos, ends):
    routed_rows = query_rows.shape[0]
    query_group = QUERY_HEADS // KEY_VALUE_HEADS
    q_doc = doc_index(q_pos, ends)
    k_doc = doc_index(k_pos, ends)
    allowed = (k_pos[None, :] <= q_pos[:, None]) & (q_doc[:, None] == k_doc[None, :]) & (k_pos[None, :] >= 0)
    query_head_rows = query_rows.reshape(routed_rows, KEY_VALUE_HEADS, query_group, HEAD_WIDTH)
    results = []
    for head_number in range(KEY_VALUE_HEADS):
        q_part = query_head_rows[:, head_number].astype(jnp.float32)
        k_part = k_win[:, head_number * HEAD_WIDTH:(head_number + 1) * HEAD_WIDTH].astype(jnp.float32)
        v_part = v_win[:, head_number * HEAD_WIDTH:(head_number + 1) * HEAD_WIDTH].astype(jnp.float32)
        scores = jnp.einsum("tgd,wd->gtw", q_part, k_part) * (1.0 / (HEAD_WIDTH ** 0.5))
        scores = jnp.where(allowed[None], scores, masked_value)
        top = jnp.max(scores, axis=-1, keepdims=True)
        weight = jnp.exp(scores - top)
        total = jnp.sum(weight, axis=-1, keepdims=True)
        rounded = weight.astype(jnp.bfloat16).astype(jnp.float32)
        mixed = jnp.einsum("gtw,wd->tgd", rounded, v_part) / jnp.transpose(total, (1, 0, 2))
        results.append(mixed.reshape(routed_rows, query_group * HEAD_WIDTH))
    return jnp.concatenate(results, axis=1).astype(jnp.bfloat16)


def reference(queries, keys, values, doc_lengths, loader_pos):
    packed_q = jnp.zeros_like(queries).at[loader_pos].set(queries)
    packed_key_rows = jnp.zeros_like(keys).at[loader_pos].set(keys)
    packed_value_rows = jnp.zeros_like(values).at[loader_pos].set(values)
    ends = jnp.cumsum(doc_lengths).astype(jnp.int32)
    padded_keys = jnp.concatenate([jnp.zeros((LONGEST_DOCUMENT, KEY_VALUE_HEADS * HEAD_WIDTH), keys.dtype), packed_key_rows], axis=0)
    padded_values = jnp.concatenate([jnp.zeros((LONGEST_DOCUMENT, KEY_VALUE_HEADS * HEAD_WIDTH), values.dtype), packed_value_rows], axis=0)

    def block(index):
        start = (index * TOK_DEV).astype(jnp.int32)
        query_rows = lax.dynamic_slice_in_dim(packed_q, start, TOK_DEV, 0)
        k_win = lax.dynamic_slice_in_dim(padded_keys, start, LONGEST_DOCUMENT + TOK_DEV, 0)
        v_win = lax.dynamic_slice_in_dim(padded_values, start, LONGEST_DOCUMENT + TOK_DEV, 0)
        q_pos = start + jnp.arange(TOK_DEV, dtype=jnp.int32)
        k_pos = start - LONGEST_DOCUMENT + jnp.arange(LONGEST_DOCUMENT + TOK_DEV, dtype=jnp.int32)
        return attend(query_rows, k_win, v_win, q_pos, k_pos, ends)

    packed_out = lax.map(block, jnp.arange(N_CTX, dtype=jnp.int32)).reshape(PACKED_TOKENS, QUERY_HEADS * HEAD_WIDTH)
    return packed_out[loader_pos]
```

```python
import jax
import jax.numpy as jnp
from jax import lax
from jax.experimental import pallas as pl
from jax.experimental.pallas import tpu as pltpu
from jax.sharding import PartitionSpec as P

KEY_VALUE_HEADS = 4
HEAD_WIDTH = 128
REACH = 2
GATHER_SHARDS = 8


masked_value = -1e30
EXP2_SCALE = 1.4426950408889634 / HEAD_WIDTH**0.5


def shifted(block, axis, distance):
    devices = range(lax.axis_size(axis))
    route = [(i - distance, i) for i in devices if i - distance in devices]
    return lax.ppermute(block, axis, route)


def doc_index(positions, ends):
    return jnp.sum((positions[:, None] >= ends[None, :]).astype(jnp.int32), axis=1)


def attend(query_rows, k_win, v_win, q_pos, k_pos, ends):
    routed_rows = query_rows.shape[0]
    query_group = query_rows.shape[1] // (KEY_VALUE_HEADS * HEAD_WIDTH)
    q_doc = doc_index(q_pos, ends)
    k_doc = doc_index(k_pos, ends)
    allowed = (
        (k_pos[None, :] <= q_pos[:, None])
        & (q_doc[:, None] == k_doc[None, :])
        & (k_pos[None, :] >= 0)
    )
    query_head_rows = query_rows.reshape(routed_rows, KEY_VALUE_HEADS, query_group, HEAD_WIDTH)
    results = []
    for head_number in range(KEY_VALUE_HEADS):
        k_part = k_win[:, head_number * HEAD_WIDTH : (head_number + 1) * HEAD_WIDTH]
        v_part = v_win[:, head_number * HEAD_WIDTH : (head_number + 1) * HEAD_WIDTH]
        scores = jnp.einsum(
            "tgd,wd->gtw",
            query_head_rows[:, head_number],
            k_part,
            preferred_element_type=jnp.float32,
        ) * (1.0 / HEAD_WIDTH**0.5)
        scores = jnp.where(allowed[None], scores, masked_value)
        top = jnp.max(scores, axis=-1, keepdims=True)
        weight = jnp.exp(scores - top)
        total = jnp.sum(weight, axis=-1, keepdims=True)
        rounded = weight.astype(jnp.bfloat16)
        mixed = jnp.einsum(
            "gtw,wd->tgd", rounded, v_part, preferred_element_type=jnp.float32
        ) / jnp.transpose(total, (1, 0, 2))
        results.append(mixed.reshape(routed_rows, query_group * HEAD_WIDTH))
    return jnp.concatenate(results, axis=1).astype(jnp.bfloat16)


def routed(queries, keys, values, doc_lengths, loader_pos):
    routed_rows = queries.shape[0]
    shards = lax.axis_size("ctx")
    cap_rows = routed_rows // shards
    shard_index = lax.axis_index("ctx")
    first_row = shard_index * routed_rows
    window = (REACH + 1) * routed_rows
    order = jnp.argsort(loader_pos)
    send_q = queries[order].reshape(shards, cap_rows, -1)
    send_k = keys[order].reshape(shards, cap_rows, -1)
    send_v = values[order].reshape(shards, cap_rows, -1)
    send_pos = loader_pos[order].reshape(shards, cap_rows)
    got_q, got_k, got_v, got_pos = (
        lax.all_to_all(send_q, "ctx", split_axis=0, concat_axis=0, tiled=True),
        lax.all_to_all(send_k, "ctx", split_axis=0, concat_axis=0, tiled=True),
        lax.all_to_all(send_v, "ctx", split_axis=0, concat_axis=0, tiled=True),
        lax.all_to_all(send_pos, "ctx", split_axis=0, concat_axis=0, tiled=True),
    )
    local = (got_pos.reshape(-1) - first_row).astype(jnp.int32)
    place = jnp.argsort(local)
    own_q = got_q.reshape(routed_rows, -1)[place]
    own_k = got_k.reshape(routed_rows, -1)[place]
    own_v = got_v.reshape(routed_rows, -1)[place]
    pieces_k = []
    pieces_v = []
    for step in range(REACH, 0, -1):
        far_k, far_v = shifted((own_k, own_v), "ctx", step)
        pieces_k.append(far_k)
        pieces_v.append(far_v)
    win_k = jnp.concatenate(pieces_k + [own_k], axis=0)
    win_v = jnp.concatenate(pieces_v + [own_v], axis=0)
    ends = jnp.cumsum(doc_lengths)
    q_pos = first_row + jnp.arange(routed_rows, dtype=jnp.int32)
    k_pos = first_row - REACH * routed_rows + jnp.arange(window, dtype=jnp.int32)
    packed_out = attend(own_q, win_k, win_v, q_pos, k_pos, ends)
    outgoing = packed_out[local].reshape(shards, cap_rows, -1)
    returned = lax.all_to_all(outgoing, "ctx", split_axis=0, concat_axis=0, tiled=True).reshape(
        routed_rows, -1
    )
    return returned[jnp.argsort(order)]


def gathered_kernel(shards, doc_ref, pos_ref, q_ref, *refs):
    k_refs, v_refs = refs[:shards], refs[shards : 2 * shards]
    out_ref, bias_ref = refs[2 * shards :]
    rows = q_ref.shape[0]
    group = q_ref.shape[1] // (KEY_VALUE_HEADS * HEAD_WIDTH)

    own = pos_ref[0:1, :]
    square = (rows, rows)
    diagonal = lax.broadcasted_iota(jnp.int32, square, 0) == lax.broadcasted_iota(jnp.int32, square, 1)
    q_pos = jnp.sum(jnp.where(diagonal, own, 0), axis=1, keepdims=True)

    def next_doc(j, carry):
        end, first = carry
        end = end + doc_ref[j]
        return end, jnp.where(q_pos >= end, end, first)

    _, q_first = lax.fori_loop(
        0, doc_ref.shape[0], next_doc, (jnp.int32(0), jnp.zeros_like(q_pos)), unroll=True
    )
    for s in range(shards):
        k_pos = pos_ref[s : s + 1, :]
        allowed = (k_pos <= q_pos) & (k_pos >= q_first)
        bias_ref[:, s * rows : (s + 1) * rows] = jnp.where(allowed, 0.0, masked_value)

    for head in range(KEY_VALUE_HEADS):
        lanes = slice(head * HEAD_WIDTH, (head + 1) * HEAD_WIDTH)
        k_part = jnp.concatenate([r[:, lanes] for r in k_refs], axis=0)
        v_part = jnp.concatenate([r[:, lanes] for r in v_refs], axis=0)
        for g in range(group):
            at = (head * group + g) * HEAD_WIDTH
            q_part = q_ref[:, at : at + HEAD_WIDTH]
            scores = lax.dot_general(
                q_part, k_part, (((1,), (1,)), ((), ())), preferred_element_type=jnp.float32
            )
            scores = scores + bias_ref[...]
            top = jnp.max(scores, axis=1, keepdims=True)
            weight = jnp.exp2((scores - top) * EXP2_SCALE)
            total = jnp.sum(weight, axis=1, keepdims=True)
            mixed = jnp.dot(weight.astype(jnp.bfloat16), v_part, preferred_element_type=jnp.float32)
            out_ref[:, at : at + HEAD_WIDTH] = (mixed / total).astype(jnp.bfloat16)


def gathered(queries, keys, values, doc_lengths, loader_pos):
    shards = lax.axis_size("ctx")
    rows = queries.shape[0]

    def from_peer(x, distance):
        return lax.ppermute(x, "ctx", [(i, i ^ distance) for i in range(shards)])

    pos = loader_pos.reshape(1, rows)
    ks, vs = {0: keys}, {0: values}
    for far in range(2, shards, 2):
        ks[far], vs[far] = from_peer(keys, far), from_peer(values, far)
    for near in range(0, shards, 2):
        ks[near + 1], vs[near + 1] = from_peer(ks[near], 1), from_peer(vs[near], 1)
    spread = lax.all_to_all(
        jnp.broadcast_to(pos, (shards, rows)), "ctx", split_axis=0, concat_axis=0, tiled=True
    )
    me = lax.axis_index("ctx")
    poss = spread[me ^ jnp.arange(shards)]
    vmem = pl.BlockSpec(memory_space=pltpu.VMEM)
    return pl.pallas_call(
        lambda *refs: gathered_kernel(shards, *refs),
        out_shape=jax.ShapeDtypeStruct(queries.shape, jnp.bfloat16),
        in_specs=[pl.BlockSpec(memory_space=pltpu.SMEM)] + [vmem] * (2 + 2 * shards),
        out_specs=vmem,
        scratch_shapes=[pltpu.VMEM((rows, shards * rows), jnp.float32)],
        compiler_params=pltpu.CompilerParams(vmem_limit_bytes=32 << 20),
    )(doc_lengths, poss, queries, *[ks[s] for s in range(shards)], *[vs[s] for s in range(shards)])


def on_device(queries, keys, values, doc_lengths, loader_pos):
    shards = lax.axis_size("ctx")
    if 2 <= shards <= GATHER_SHARDS and shards & (shards - 1) == 0:
        return gathered(queries, keys, values, doc_lengths, loader_pos)
    return routed(queries, keys, values, doc_lengths, loader_pos)


def solution(mesh):
    placed = (
        P(("grp", "ctx"), None),
        P(("grp", "ctx"), None),
        P(("grp", "ctx"), None),
        P("grp"),
        P(("grp", "ctx")),
    )
    return jax.shard_map(
        on_device, mesh=mesh, in_specs=placed, out_specs=P(("grp", "ctx"), None), check_vma=False
    )
```

```python
import jax
import jax.numpy as jnp
from jax import lax
from jax.experimental import pallas as pl
from jax.experimental.pallas import tpu as pltpu
from jax.sharding import PartitionSpec as P

KEY_VALUE_HEADS = 4
HEAD_WIDTH = 128
REACH = 2
GATHER_SHARDS = 8
POS_ROWS = 8


masked_value = -1e30
EXP2_SCALE = 1.4426950408889634 / HEAD_WIDTH**0.5


def shifted(block, axis, distance):
    devices = range(lax.axis_size(axis))
    route = [(i - distance, i) for i in devices if i - distance in devices]
    return lax.ppermute(block, axis, route)


def doc_index(positions, ends):
    return jnp.sum((positions[:, None] >= ends[None, :]).astype(jnp.int32), axis=1)


def attend(query_rows, k_win, v_win, q_pos, k_pos, ends):
    routed_rows = query_rows.shape[0]
    query_group = query_rows.shape[1] // (KEY_VALUE_HEADS * HEAD_WIDTH)
    q_doc = doc_index(q_pos, ends)
    k_doc = doc_index(k_pos, ends)
    allowed = (
        (k_pos[None, :] <= q_pos[:, None])
        & (q_doc[:, None] == k_doc[None, :])
        & (k_pos[None, :] >= 0)
    )
    query_head_rows = query_rows.reshape(routed_rows, KEY_VALUE_HEADS, query_group, HEAD_WIDTH)
    results = []
    for head_number in range(KEY_VALUE_HEADS):
        k_part = k_win[:, head_number * HEAD_WIDTH : (head_number + 1) * HEAD_WIDTH]
        v_part = v_win[:, head_number * HEAD_WIDTH : (head_number + 1) * HEAD_WIDTH]
        scores = jnp.einsum(
            "tgd,wd->gtw",
            query_head_rows[:, head_number],
            k_part,
            preferred_element_type=jnp.float32,
        ) * (1.0 / HEAD_WIDTH**0.5)
        scores = jnp.where(allowed[None], scores, masked_value)
        top = jnp.max(scores, axis=-1, keepdims=True)
        weight = jnp.exp(scores - top)
        total = jnp.sum(weight, axis=-1, keepdims=True)
        rounded = weight.astype(jnp.bfloat16)
        mixed = jnp.einsum(
            "gtw,wd->tgd", rounded, v_part, preferred_element_type=jnp.float32
        ) / jnp.transpose(total, (1, 0, 2))
        results.append(mixed.reshape(routed_rows, query_group * HEAD_WIDTH))
    return jnp.concatenate(results, axis=1).astype(jnp.bfloat16)


def routed(queries, keys, values, doc_lengths, loader_pos):
    routed_rows = queries.shape[0]
    shards = lax.axis_size("ctx")
    cap_rows = routed_rows // shards
    shard_index = lax.axis_index("ctx")
    first_row = shard_index * routed_rows
    window = (REACH + 1) * routed_rows
    order = jnp.argsort(loader_pos)
    send_q = queries[order].reshape(shards, cap_rows, -1)
    send_k = keys[order].reshape(shards, cap_rows, -1)
    send_v = values[order].reshape(shards, cap_rows, -1)
    send_pos = loader_pos[order].reshape(shards, cap_rows)
    got_q, got_k, got_v, got_pos = (
        lax.all_to_all(send_q, "ctx", split_axis=0, concat_axis=0, tiled=True),
        lax.all_to_all(send_k, "ctx", split_axis=0, concat_axis=0, tiled=True),
        lax.all_to_all(send_v, "ctx", split_axis=0, concat_axis=0, tiled=True),
        lax.all_to_all(send_pos, "ctx", split_axis=0, concat_axis=0, tiled=True),
    )
    local = (got_pos.reshape(-1) - first_row).astype(jnp.int32)
    place = jnp.argsort(local)
    own_q = got_q.reshape(routed_rows, -1)[place]
    own_k = got_k.reshape(routed_rows, -1)[place]
    own_v = got_v.reshape(routed_rows, -1)[place]
    pieces_k = []
    pieces_v = []
    for step in range(REACH, 0, -1):
        far_k, far_v = shifted((own_k, own_v), "ctx", step)
        pieces_k.append(far_k)
        pieces_v.append(far_v)
    win_k = jnp.concatenate(pieces_k + [own_k], axis=0)
    win_v = jnp.concatenate(pieces_v + [own_v], axis=0)
    ends = jnp.cumsum(doc_lengths)
    q_pos = first_row + jnp.arange(routed_rows, dtype=jnp.int32)
    k_pos = first_row - REACH * routed_rows + jnp.arange(window, dtype=jnp.int32)
    packed_out = attend(own_q, win_k, win_v, q_pos, k_pos, ends)
    outgoing = packed_out[local].reshape(shards, cap_rows, -1)
    returned = lax.all_to_all(outgoing, "ctx", split_axis=0, concat_axis=0, tiled=True).reshape(
        routed_rows, -1
    )
    return returned[jnp.argsort(order)]


def lanes(head):
    return slice(head * HEAD_WIDTH, (head + 1) * HEAD_WIDTH)


def after(x, *earlier):
    return lax.optimization_barrier((x, *earlier))[0]


def pack_kernel(k_ref, v_ref, pos_ref, out_ref, pos_vmem, sems):
    rows = k_ref.shape[0]
    copies = [pltpu.make_async_copy(pos_ref, pos_vmem, sems.at[2 * KEY_VALUE_HEADS])]
    for i, ref in enumerate((k_ref, v_ref)):
        for head in range(KEY_VALUE_HEADS):
            slab = i * KEY_VALUE_HEADS + head
            copies.append(
                pltpu.make_async_copy(
                    ref.at[:, lanes(head)], out_ref.at[slab * rows : (slab + 1) * rows, :], sems.at[slab]
                )
            )
    for copy in copies:
        copy.start()
    copies[0].wait()
    pos = pos_vmem[...]
    row = lax.broadcasted_iota(jnp.int32, (POS_ROWS, rows), 0)
    digits = jnp.where(row == 0, pos % 128, pos // 128)
    out_ref[2 * KEY_VALUE_HEADS * rows :, :] = digits.astype(jnp.float32).astype(jnp.bfloat16)
    for copy in copies[1:]:
        copy.wait()


def positions(block_ref):
    at = block_ref.shape[0] - POS_ROWS
    both = block_ref[at:, :].astype(jnp.float32)
    return both[0:1] + 128.0 * both[1:2]


def keys_of(block_refs, rows, head):
    return jnp.concatenate([r[head * rows : (head + 1) * rows, :] for r in block_refs], axis=0)


def values_of(block_refs, rows, head):
    return keys_of(block_refs, rows, KEY_VALUE_HEADS + head)


def write_bias(bias_ref, block_refs, q_pos, q_first):
    rows = bias_ref.shape[0]
    for s, ref in enumerate(block_refs):
        k_pos = positions(ref)
        allowed = (k_pos <= q_pos) & (k_pos >= q_first)
        bias_ref[:, s * rows : (s + 1) * rows] = jnp.where(allowed, 0.0, masked_value)


def stacked(ref, head, group):
    return jnp.concatenate([ref[:, lanes(head * group + g)] for g in range(group)], axis=0)


def fold_kernel(shards, first, last, *refs):
    if first:
        (doc_ref, q_ref), refs = refs[:2], refs[2:]
    else:
        (q_ref, where_ref, mean_ref, level_ref), refs = refs[:4], refs[4:]
    block_refs, refs = refs[:shards], refs[shards:]
    outs, (bias_ref, weight_ref) = refs[:-2], refs[-2:]
    rows = q_ref.shape[0]
    group = q_ref.shape[1] // HEAD_WIDTH // KEY_VALUE_HEADS
    if first:
        square = (rows, rows)
        diagonal = lax.broadcasted_iota(jnp.int32, square, 0) == lax.broadcasted_iota(jnp.int32, square, 1)
        q_pos = jnp.sum(jnp.where(diagonal, positions(block_refs[0]), 0.0), axis=1, keepdims=True)
        end, q_first = jnp.int32(0), jnp.zeros_like(q_pos)
        for j in range(doc_ref.shape[0]):
            end = end + doc_ref[j]
            limit = end.astype(jnp.float32)
            q_first = jnp.where(q_pos >= limit, limit, q_first)
        outs[0][0] = jnp.broadcast_to(q_pos, (rows, HEAD_WIDTH))
        outs[0][1] = jnp.broadcast_to(q_first, (rows, HEAD_WIDTH))
        outs = outs[1:]
    else:
        q_pos, q_first = where_ref[0], where_ref[1]
    write_bias(bias_ref, block_refs, q_pos, q_first)

    for head in range(KEY_VALUE_HEADS):
        k_part, v_part = keys_of(block_refs, rows, head), values_of(block_refs, rows, head)
        raw = lax.dot_general(
            stacked(q_ref, head, group),
            k_part,
            (((1,), (1,)), ((), ())),
            preferred_element_type=jnp.float32,
        )
        tops, totals, before = [], [], []
        for g in range(group):
            part = slice(g * rows, (g + 1) * rows)
            scores = raw[part] + bias_ref[...]
            top = jnp.max(scores, axis=1, keepdims=True)
            if first:
                weight = jnp.exp2((scores - top) * EXP2_SCALE)
                total = jnp.sum(weight, axis=1, keepdims=True)
            else:
                level = level_ref[head * group + g]
                top = jnp.maximum(top, level)
                weight = jnp.exp2((scores - jnp.tile(top, (1, shards))) * EXP2_SCALE)
                before.append(jnp.exp2((level - top) * EXP2_SCALE))
                total = before[-1] + jnp.sum(weight, axis=1, keepdims=True)
            weight_ref[part] = weight.astype(jnp.bfloat16)
            tops.append(top)
            totals.append(total)
        mixed = jnp.dot(weight_ref[...], v_part, preferred_element_type=jnp.float32)
        for g in range(group):
            q_head = head * group + g
            mean = mixed[g * rows : (g + 1) * rows]
            if not first:
                mean = mean + before[g] * mean_ref[q_head]
            mean = mean / totals[g]
            if last:
                outs[0][:, lanes(q_head)] = mean.astype(jnp.bfloat16)
            else:
                outs[0][q_head] = mean
                level = tops[g] + jnp.log2(totals[g]) * (1.0 / EXP2_SCALE)
                outs[1][q_head] = jnp.broadcast_to(level, (rows, HEAD_WIDTH))


def gathered(queries, keys, values, doc_lengths, loader_pos):
    shards = lax.axis_size("ctx")
    rows = queries.shape[0]
    heads = queries.shape[1] // HEAD_WIDTH
    vmem, smem = pl.BlockSpec(memory_space=pltpu.VMEM), pl.BlockSpec(memory_space=pltpu.SMEM)
    hbm = pl.BlockSpec(memory_space=pl.ANY)
    per_head = jax.ShapeDtypeStruct((heads, rows, HEAD_WIDTH), jnp.float32)

    def swap(x, distance):
        return lax.ppermute(x, "ctx", [(i, i ^ distance) for i in range(shards)])

    def fold(name, blocks, *state, last=False):
        n, first = len(blocks), not state
        out_shape = (per_head, per_head)
        if first:
            out_shape = (jax.ShapeDtypeStruct((2, rows, HEAD_WIDTH), jnp.float32), *out_shape)
        if last:
            out_shape = (jax.ShapeDtypeStruct(queries.shape, queries.dtype),)
        return pl.pallas_call(
            lambda *refs: fold_kernel(n, first, last, *refs),
            out_shape=out_shape,
            in_specs=([smem] if first else []) + [vmem] * (1 + len(state) + n),
            out_specs=(vmem,) * len(out_shape),
            scratch_shapes=[
                pltpu.VMEM((rows, n * rows), jnp.float32),
                pltpu.VMEM((heads // KEY_VALUE_HEADS * rows, n * rows), jnp.bfloat16),
            ],
            compiler_params=pltpu.CompilerParams(vmem_limit_bytes=32 << 20),
            name=name,
        )(*([doc_lengths] if first else []), queries, *state, *blocks)

    slabs = 2 * KEY_VALUE_HEADS
    own = pl.pallas_call(
        pack_kernel,
        out_shape=jax.ShapeDtypeStruct((slabs * rows + POS_ROWS, HEAD_WIDTH), keys.dtype),
        in_specs=[hbm, hbm, hbm],
        out_specs=vmem,
        scratch_shapes=[
            pltpu.VMEM((1, rows), jnp.int32),
            pltpu.SemaphoreType.DMA((slabs + 1,)),
        ],
        name="pack",
    )(keys, values, loader_pos.reshape(1, rows))
    six = swap(own, 6)
    two = swap(own, 2)
    four = swap(six, 2)
    where, *state = fold("early", [own, six, two, swap(after(own, six), 1), swap(six, 1)])
    four = after(four, *state)
    state = fold("middle", [swap(two, 1), four], where, *state)
    return fold("last", [swap(four, 1)], where, *state, last=True)[0]


def on_device(queries, keys, values, doc_lengths, loader_pos):
    shards = lax.axis_size("ctx")
    if shards == GATHER_SHARDS:
        return gathered(queries, keys, values, doc_lengths, loader_pos)
    return routed(queries, keys, values, doc_lengths, loader_pos)


def solution(mesh):
    placed = (
        P(("grp", "ctx"), None),
        P(("grp", "ctx"), None),
        P(("grp", "ctx"), None),
        P("grp"),
        P(("grp", "ctx")),
    )
    return jax.shard_map(
        on_device, mesh=mesh, in_specs=placed, out_specs=P(("grp", "ctx"), None), check_vma=False
    )
```

```python
import jax
import jax.numpy as jnp
from jax import lax
from jax.experimental import pallas as pl
from jax.experimental.pallas import tpu as pltpu
from jax.sharding import PartitionSpec as P

KEY_VALUE_HEADS = 4
HEAD_WIDTH = 128
REACH = 2
GATHER_SHARDS = 8
POS_ROWS = 8


masked_value = -1e30
EXP2_SCALE = 1.4426950408889634 / HEAD_WIDTH**0.5


def shifted(block, axis, distance):
    devices = range(lax.axis_size(axis))
    route = [(i - distance, i) for i in devices if i - distance in devices]
    return lax.ppermute(block, axis, route)


def doc_index(positions, ends):
    return jnp.sum((positions[:, None] >= ends[None, :]).astype(jnp.int32), axis=1)


def attend(query_rows, k_win, v_win, q_pos, k_pos, ends):
    routed_rows = query_rows.shape[0]
    query_group = query_rows.shape[1] // (KEY_VALUE_HEADS * HEAD_WIDTH)
    q_doc = doc_index(q_pos, ends)
    k_doc = doc_index(k_pos, ends)
    allowed = (
        (k_pos[None, :] <= q_pos[:, None])
        & (q_doc[:, None] == k_doc[None, :])
        & (k_pos[None, :] >= 0)
    )
    query_head_rows = query_rows.reshape(routed_rows, KEY_VALUE_HEADS, query_group, HEAD_WIDTH)
    results = []
    for head_number in range(KEY_VALUE_HEADS):
        k_part = k_win[:, head_number * HEAD_WIDTH : (head_number + 1) * HEAD_WIDTH]
        v_part = v_win[:, head_number * HEAD_WIDTH : (head_number + 1) * HEAD_WIDTH]
        scores = jnp.einsum(
            "tgd,wd->gtw",
            query_head_rows[:, head_number],
            k_part,
            preferred_element_type=jnp.float32,
        ) * (1.0 / HEAD_WIDTH**0.5)
        scores = jnp.where(allowed[None], scores, masked_value)
        top = jnp.max(scores, axis=-1, keepdims=True)
        weight = jnp.exp(scores - top)
        total = jnp.sum(weight, axis=-1, keepdims=True)
        rounded = weight.astype(jnp.bfloat16)
        mixed = jnp.einsum(
            "gtw,wd->tgd", rounded, v_part, preferred_element_type=jnp.float32
        ) / jnp.transpose(total, (1, 0, 2))
        results.append(mixed.reshape(routed_rows, query_group * HEAD_WIDTH))
    return jnp.concatenate(results, axis=1).astype(jnp.bfloat16)


def routed(queries, keys, values, doc_lengths, loader_pos):
    routed_rows = queries.shape[0]
    shards = lax.axis_size("ctx")
    cap_rows = routed_rows // shards
    shard_index = lax.axis_index("ctx")
    first_row = shard_index * routed_rows
    window = (REACH + 1) * routed_rows
    order = jnp.argsort(loader_pos)
    send_q = queries[order].reshape(shards, cap_rows, -1)
    send_k = keys[order].reshape(shards, cap_rows, -1)
    send_v = values[order].reshape(shards, cap_rows, -1)
    send_pos = loader_pos[order].reshape(shards, cap_rows)
    got_q, got_k, got_v, got_pos = (
        lax.all_to_all(send_q, "ctx", split_axis=0, concat_axis=0, tiled=True),
        lax.all_to_all(send_k, "ctx", split_axis=0, concat_axis=0, tiled=True),
        lax.all_to_all(send_v, "ctx", split_axis=0, concat_axis=0, tiled=True),
        lax.all_to_all(send_pos, "ctx", split_axis=0, concat_axis=0, tiled=True),
    )
    local = (got_pos.reshape(-1) - first_row).astype(jnp.int32)
    place = jnp.argsort(local)
    own_q = got_q.reshape(routed_rows, -1)[place]
    own_k = got_k.reshape(routed_rows, -1)[place]
    own_v = got_v.reshape(routed_rows, -1)[place]
    pieces_k = []
    pieces_v = []
    for step in range(REACH, 0, -1):
        far_k, far_v = shifted((own_k, own_v), "ctx", step)
        pieces_k.append(far_k)
        pieces_v.append(far_v)
    win_k = jnp.concatenate(pieces_k + [own_k], axis=0)
    win_v = jnp.concatenate(pieces_v + [own_v], axis=0)
    ends = jnp.cumsum(doc_lengths)
    q_pos = first_row + jnp.arange(routed_rows, dtype=jnp.int32)
    k_pos = first_row - REACH * routed_rows + jnp.arange(window, dtype=jnp.int32)
    packed_out = attend(own_q, win_k, win_v, q_pos, k_pos, ends)
    outgoing = packed_out[local].reshape(shards, cap_rows, -1)
    returned = lax.all_to_all(outgoing, "ctx", split_axis=0, concat_axis=0, tiled=True).reshape(
        routed_rows, -1
    )
    return returned[jnp.argsort(order)]


def lanes(head):
    return slice(head * HEAD_WIDTH, (head + 1) * HEAD_WIDTH)


def after(x, *earlier):
    return lax.optimization_barrier((x, *earlier))[0]


def pack_kernel(k_ref, v_ref, pos_ref, out_ref, pos_vmem, sems):
    rows = k_ref.shape[0]
    copies = [pltpu.make_async_copy(pos_ref, pos_vmem, sems.at[2 * KEY_VALUE_HEADS])]
    for i, ref in enumerate((k_ref, v_ref)):
        for head in range(KEY_VALUE_HEADS):
            slab = i * KEY_VALUE_HEADS + head
            copies.append(
                pltpu.make_async_copy(
                    ref.at[:, lanes(head)], out_ref.at[slab * rows : (slab + 1) * rows, :], sems.at[slab]
                )
            )
    for copy in copies:
        copy.start()
    copies[0].wait()
    pos = pos_vmem[...]
    row = lax.broadcasted_iota(jnp.int32, (POS_ROWS, rows), 0)
    digits = jnp.where(row == 0, pos % 128, pos // 128)
    out_ref[2 * KEY_VALUE_HEADS * rows :, :] = digits.astype(jnp.float32).astype(jnp.bfloat16)
    for copy in copies[1:]:
        copy.wait()


def positions(block_ref):
    at = block_ref.shape[0] - POS_ROWS
    both = block_ref[at:, :].astype(jnp.float32)
    return both[0:1] + 128.0 * both[1:2]


def keys_of(block_refs, rows, head):
    return jnp.concatenate([r[head * rows : (head + 1) * rows, :] for r in block_refs], axis=0)


def values_of(block_refs, rows, head):
    return keys_of(block_refs, rows, KEY_VALUE_HEADS + head)


def write_bias(bias_ref, block_refs, q_pos, q_first):
    rows = bias_ref.shape[0]
    for s, ref in enumerate(block_refs):
        k_pos = positions(ref)
        allowed = (k_pos <= q_pos) & (k_pos >= q_first)
        bias_ref[:, s * rows : (s + 1) * rows] = jnp.where(allowed, 0.0, masked_value)


def stacked(ref, head, group):
    return jnp.concatenate([ref[:, lanes(head * group + g)] for g in range(group)], axis=0)


def fold_kernel(shards, first, last, *refs):
    if first:
        (doc_ref, q_ref), refs = refs[:2], refs[2:]
    else:
        (q_ref, where_ref, mean_ref, level_ref), refs = refs[:4], refs[4:]
    block_refs, refs = refs[:shards], refs[shards:]
    if last:
        out_hbm, bias_ref, weight_ref, out_ref, sems = refs
        outs, stores = (out_ref,), []
    else:
        outs, (bias_ref, weight_ref) = refs[:-2], refs[-2:]
    rows = q_ref.shape[0]
    group = q_ref.shape[1] // HEAD_WIDTH // KEY_VALUE_HEADS
    if first:
        square = (rows, rows)
        diagonal = lax.broadcasted_iota(jnp.int32, square, 0) == lax.broadcasted_iota(jnp.int32, square, 1)
        q_pos = jnp.sum(jnp.where(diagonal, positions(block_refs[0]), 0.0), axis=1, keepdims=True)
        end, q_first = jnp.int32(0), jnp.zeros_like(q_pos)
        for j in range(doc_ref.shape[0]):
            end = end + doc_ref[j]
            limit = end.astype(jnp.float32)
            q_first = jnp.where(q_pos >= limit, limit, q_first)
        outs[0][0] = jnp.broadcast_to(q_pos, (rows, HEAD_WIDTH))
        outs[0][1] = jnp.broadcast_to(q_first, (rows, HEAD_WIDTH))
        outs = outs[1:]
    else:
        q_pos, q_first = where_ref[0], where_ref[1]
    write_bias(bias_ref, block_refs, q_pos, q_first)

    for head in range(KEY_VALUE_HEADS):
        k_part, v_part = keys_of(block_refs, rows, head), values_of(block_refs, rows, head)
        raw = lax.dot_general(
            stacked(q_ref, head, group),
            k_part,
            (((1,), (1,)), ((), ())),
            preferred_element_type=jnp.float32,
        )
        tops, totals, before = [], [], []
        for g in range(group):
            part = slice(g * rows, (g + 1) * rows)
            scores = raw[part] + bias_ref[...]
            top = jnp.max(scores, axis=1, keepdims=True)
            if first:
                weight = jnp.exp2((scores - top) * EXP2_SCALE)
                total = jnp.sum(weight, axis=1, keepdims=True)
            else:
                level = level_ref[head * group + g]
                top = jnp.maximum(top, level)
                weight = jnp.exp2((scores - jnp.tile(top, (1, shards))) * EXP2_SCALE)
                before.append(jnp.exp2((level - top) * EXP2_SCALE))
                total = before[-1] + jnp.sum(weight, axis=1, keepdims=True)
            weight_ref[part] = weight.astype(jnp.bfloat16)
            tops.append(top)
            totals.append(total)
        mixed = jnp.dot(weight_ref[...], v_part, preferred_element_type=jnp.float32)
        for g in range(group):
            q_head = head * group + g
            mean = mixed[g * rows : (g + 1) * rows]
            if not first:
                mean = mean + before[g] * mean_ref[q_head]
            mean = mean * (1.0 / totals[g])
            if last:
                outs[0][:, lanes(q_head)] = mean.astype(jnp.bfloat16)
            else:
                outs[0][q_head] = mean
                level = tops[g] + jnp.log2(totals[g]) * (1.0 / EXP2_SCALE)
                outs[1][q_head] = jnp.broadcast_to(level, (rows, HEAD_WIDTH))
        if last:
            done = slice(head * group * HEAD_WIDTH, (head + 1) * group * HEAD_WIDTH)
            stores.append(
                pltpu.make_async_copy(out_ref.at[:, done], out_hbm.at[:, done], sems.at[head])
            )
            stores[-1].start()
    if last:
        for store in stores:
            store.wait()


def gathered(queries, keys, values, doc_lengths, loader_pos):
    shards = lax.axis_size("ctx")
    rows = queries.shape[0]
    heads = queries.shape[1] // HEAD_WIDTH
    vmem, smem = pl.BlockSpec(memory_space=pltpu.VMEM), pl.BlockSpec(memory_space=pltpu.SMEM)
    hbm = pl.BlockSpec(memory_space=pl.ANY)
    per_head = jax.ShapeDtypeStruct((heads, rows, HEAD_WIDTH), jnp.float32)

    def swap(x, distance):
        return lax.ppermute(x, "ctx", [(i, i ^ distance) for i in range(shards)])

    def fold(name, blocks, *state, last=False):
        n, first = len(blocks), not state
        out_shape = (per_head, per_head)
        if first:
            out_shape = (jax.ShapeDtypeStruct((2, rows, HEAD_WIDTH), jnp.float32), *out_shape)
        if last:
            out_shape = (jax.ShapeDtypeStruct(queries.shape, queries.dtype),)
        return pl.pallas_call(
            lambda *refs: fold_kernel(n, first, last, *refs),
            out_shape=out_shape,
            in_specs=([smem] if first else []) + [vmem] * (1 + len(state) + n),
            out_specs=(hbm if last else vmem,) * len(out_shape),
            scratch_shapes=[
                pltpu.VMEM((rows, n * rows), jnp.float32),
                pltpu.VMEM((heads // KEY_VALUE_HEADS * rows, n * rows), jnp.bfloat16),
            ]
            + last
            * [
                pltpu.VMEM(queries.shape, queries.dtype),
                pltpu.SemaphoreType.DMA((KEY_VALUE_HEADS,)),
            ],
            compiler_params=pltpu.CompilerParams(vmem_limit_bytes=32 << 20),
            name=name,
        )(*([doc_lengths] if first else []), queries, *state, *blocks)

    slabs = 2 * KEY_VALUE_HEADS
    own = pl.pallas_call(
        pack_kernel,
        out_shape=pltpu.VMEM((slabs * rows + POS_ROWS, HEAD_WIDTH), keys.dtype),
        in_specs=[hbm, hbm, hbm],
        out_specs=vmem,
        scratch_shapes=[
            pltpu.VMEM((1, rows), jnp.int32),
            pltpu.SemaphoreType.DMA((slabs + 1,)),
        ],
        name="pack",
    )(keys, values, loader_pos.reshape(1, rows))
    six = swap(own, 6)
    two = swap(own, 2)
    four = swap(six, 2)
    where, *state = fold("early", [own, six, two, swap(after(own, six), 1), swap(six, 1)])
    four = after(four, *state)
    state = fold("middle", [swap(two, 1), four], where, *state)
    return fold("last", [swap(four, 1)], where, *state, last=True)[0]


def on_device(queries, keys, values, doc_lengths, loader_pos):
    shards = lax.axis_size("ctx")
    if shards == GATHER_SHARDS:
        return gathered(queries, keys, values, doc_lengths, loader_pos)
    return routed(queries, keys, values, doc_lengths, loader_pos)


def solution(mesh):
    placed = (
        P(("grp", "ctx"), None),
        P(("grp", "ctx"), None),
        P(("grp", "ctx"), None),
        P("grp"),
        P(("grp", "ctx")),
    )
    return jax.shard_map(
        on_device, mesh=mesh, in_specs=placed, out_specs=P(("grp", "ctx"), None), check_vma=False
    )
```

```python
import jax
import jax.numpy as jnp
from jax import lax
from jax.experimental import pallas as pl
from jax.experimental.pallas import tpu as pltpu
from jax.sharding import PartitionSpec as P

KEY_VALUE_HEADS = 4
HEAD_WIDTH = 128
REACH = 2
GATHER_SHARDS = 8
POS_ROWS = 8


masked_value = -1e30
EXP2_SCALE = 1.4426950408889634 / HEAD_WIDTH**0.5


def shifted(block, axis, distance):
    devices = range(lax.axis_size(axis))
    route = [(i - distance, i) for i in devices if i - distance in devices]
    return lax.ppermute(block, axis, route)


def doc_index(positions, ends):
    return jnp.sum((positions[:, None] >= ends[None, :]).astype(jnp.int32), axis=1)


def attend(query_rows, k_win, v_win, q_pos, k_pos, ends):
    routed_rows = query_rows.shape[0]
    query_group = query_rows.shape[1] // (KEY_VALUE_HEADS * HEAD_WIDTH)
    q_doc = doc_index(q_pos, ends)
    k_doc = doc_index(k_pos, ends)
    allowed = (
        (k_pos[None, :] <= q_pos[:, None])
        & (q_doc[:, None] == k_doc[None, :])
        & (k_pos[None, :] >= 0)
    )
    query_head_rows = query_rows.reshape(routed_rows, KEY_VALUE_HEADS, query_group, HEAD_WIDTH)
    results = []
    for head_number in range(KEY_VALUE_HEADS):
        k_part = k_win[:, head_number * HEAD_WIDTH : (head_number + 1) * HEAD_WIDTH]
        v_part = v_win[:, head_number * HEAD_WIDTH : (head_number + 1) * HEAD_WIDTH]
        scores = jnp.einsum(
            "tgd,wd->gtw",
            query_head_rows[:, head_number],
            k_part,
            preferred_element_type=jnp.float32,
        ) * (1.0 / HEAD_WIDTH**0.5)
        scores = jnp.where(allowed[None], scores, masked_value)
        top = jnp.max(scores, axis=-1, keepdims=True)
        weight = jnp.exp(scores - top)
        total = jnp.sum(weight, axis=-1, keepdims=True)
        rounded = weight.astype(jnp.bfloat16)
        mixed = jnp.einsum(
            "gtw,wd->tgd", rounded, v_part, preferred_element_type=jnp.float32
        ) / jnp.transpose(total, (1, 0, 2))
        results.append(mixed.reshape(routed_rows, query_group * HEAD_WIDTH))
    return jnp.concatenate(results, axis=1).astype(jnp.bfloat16)


def routed(queries, keys, values, doc_lengths, loader_pos):
    routed_rows = queries.shape[0]
    shards = lax.axis_size("ctx")
    cap_rows = routed_rows // shards
    shard_index = lax.axis_index("ctx")
    first_row = shard_index * routed_rows
    window = (REACH + 1) * routed_rows
    order = jnp.argsort(loader_pos)
    send_q = queries[order].reshape(shards, cap_rows, -1)
    send_k = keys[order].reshape(shards, cap_rows, -1)
    send_v = values[order].reshape(shards, cap_rows, -1)
    send_pos = loader_pos[order].reshape(shards, cap_rows)
    got_q, got_k, got_v, got_pos = (
        lax.all_to_all(send_q, "ctx", split_axis=0, concat_axis=0, tiled=True),
        lax.all_to_all(send_k, "ctx", split_axis=0, concat_axis=0, tiled=True),
        lax.all_to_all(send_v, "ctx", split_axis=0, concat_axis=0, tiled=True),
        lax.all_to_all(send_pos, "ctx", split_axis=0, concat_axis=0, tiled=True),
    )
    local = (got_pos.reshape(-1) - first_row).astype(jnp.int32)
    place = jnp.argsort(local)
    own_q = got_q.reshape(routed_rows, -1)[place]
    own_k = got_k.reshape(routed_rows, -1)[place]
    own_v = got_v.reshape(routed_rows, -1)[place]
    pieces_k = []
    pieces_v = []
    for step in range(REACH, 0, -1):
        far_k, far_v = shifted((own_k, own_v), "ctx", step)
        pieces_k.append(far_k)
        pieces_v.append(far_v)
    win_k = jnp.concatenate(pieces_k + [own_k], axis=0)
    win_v = jnp.concatenate(pieces_v + [own_v], axis=0)
    ends = jnp.cumsum(doc_lengths)
    q_pos = first_row + jnp.arange(routed_rows, dtype=jnp.int32)
    k_pos = first_row - REACH * routed_rows + jnp.arange(window, dtype=jnp.int32)
    packed_out = attend(own_q, win_k, win_v, q_pos, k_pos, ends)
    outgoing = packed_out[local].reshape(shards, cap_rows, -1)
    returned = lax.all_to_all(outgoing, "ctx", split_axis=0, concat_axis=0, tiled=True).reshape(
        routed_rows, -1
    )
    return returned[jnp.argsort(order)]


def lanes(head):
    return slice(head * HEAD_WIDTH, (head + 1) * HEAD_WIDTH)


def after(x, *earlier):
    return lax.optimization_barrier((x, *earlier))[0]


def pack_kernel(k_ref, v_ref, pos_ref, out_ref, pos_vmem, sems):
    rows = k_ref.shape[0]
    copies = [pltpu.make_async_copy(pos_ref, pos_vmem, sems.at[2 * KEY_VALUE_HEADS])]
    for i, ref in enumerate((k_ref, v_ref)):
        for head in range(KEY_VALUE_HEADS):
            slab = i * KEY_VALUE_HEADS + head
            copies.append(
                pltpu.make_async_copy(
                    ref.at[:, lanes(head)], out_ref.at[slab * rows : (slab + 1) * rows, :], sems.at[slab]
                )
            )
    for copy in copies:
        copy.start()
    copies[0].wait()
    pos = pos_vmem[...]
    row = lax.broadcasted_iota(jnp.int32, (POS_ROWS, rows), 0)
    digits = jnp.where(row == 0, pos % 128, pos // 128)
    out_ref[2 * KEY_VALUE_HEADS * rows :, :] = digits.astype(jnp.float32).astype(jnp.bfloat16)
    for copy in copies[1:]:
        copy.wait()


def positions(block_ref):
    at = block_ref.shape[0] - POS_ROWS
    both = block_ref[at:, :].astype(jnp.float32)
    return both[0:1] + 128.0 * both[1:2]


def keys_of(block_refs, rows, head):
    return jnp.concatenate([r[head * rows : (head + 1) * rows, :] for r in block_refs], axis=0)


def values_of(block_refs, rows, head):
    return keys_of(block_refs, rows, KEY_VALUE_HEADS + head)


def write_bias(bias_ref, block_refs, q_pos, q_first):
    rows = bias_ref.shape[0]
    for s, ref in enumerate(block_refs):
        k_pos = positions(ref)
        allowed = (k_pos <= q_pos) & (k_pos >= q_first)
        bias_ref[:, s * rows : (s + 1) * rows] = jnp.where(allowed, 0.0, masked_value)


def stacked(ref, head, group):
    return jnp.concatenate([ref[:, lanes(head * group + g)] for g in range(group)], axis=0)


def fold_kernel(shards, first, last, *refs):
    if first:
        (doc_ref, q_ref), refs = refs[:2], refs[2:]
    else:
        (q_ref, where_ref, mean_ref, level_ref), refs = refs[:4], refs[4:]
    block_refs, refs = refs[:shards], refs[shards:]
    if last:
        out_hbm, bias_ref, out_ref, sems = refs
        stores = []
    else:
        outs, bias_ref = refs[:-1], refs[-1]
    rows = q_ref.shape[0]
    group = q_ref.shape[1] // HEAD_WIDTH // KEY_VALUE_HEADS

    def raw_scores(head):
        return lax.dot_general(
            stacked(q_ref, head, group),
            keys_of(block_refs, rows, head),
            (((1,), (1,)), ((), ())),
            preferred_element_type=jnp.float32,
        )

    raws = [raw_scores(0), raw_scores(1)]
    if first:
        square = (rows, rows)
        diagonal = lax.broadcasted_iota(jnp.int32, square, 0) == lax.broadcasted_iota(jnp.int32, square, 1)
        q_pos = jnp.sum(jnp.where(diagonal, positions(block_refs[0]), 0.0), axis=1, keepdims=True)
        end, q_first = jnp.int32(0), jnp.zeros_like(q_pos)
        for j in range(doc_ref.shape[0]):
            end = end + doc_ref[j]
            limit = end.astype(jnp.float32)
            q_first = jnp.where(q_pos >= limit, limit, q_first)
        outs[0][0] = jnp.broadcast_to(q_pos, (rows, HEAD_WIDTH))
        outs[0][1] = jnp.broadcast_to(q_first, (rows, HEAD_WIDTH))
        outs = outs[1:]
    else:
        q_pos, q_first = where_ref[0], where_ref[1]
    write_bias(bias_ref, block_refs, q_pos, q_first)

    def weigh(head):
        weights, tops, totals, before = [], [], [], []
        for g in range(group):
            scores = raws[head][g * rows : (g + 1) * rows] + bias_ref[...]
            top = jnp.max(scores, axis=1, keepdims=True)
            if first:
                weight = jnp.exp2((scores - top) * EXP2_SCALE)
                total = jnp.sum(weight, axis=1, keepdims=True)
            else:
                level = level_ref[head * group + g]
                top = jnp.maximum(top, level)
                weight = jnp.exp2((scores - jnp.tile(top, (1, shards))) * EXP2_SCALE)
                before.append(jnp.exp2((level - top) * EXP2_SCALE))
                total = before[-1] + jnp.sum(weight, axis=1, keepdims=True)
            weights.append(weight.astype(jnp.bfloat16))
            tops.append(top)
            totals.append(total)
        return jnp.concatenate(weights, axis=0), tops, totals, before

    def mix(head, weights, tops, totals, before):
        mixed = jnp.dot(weights, values_of(block_refs, rows, head), preferred_element_type=jnp.float32)
        for g in range(group):
            q_head = head * group + g
            mean = mixed[g * rows : (g + 1) * rows]
            if not first:
                mean = mean + before[g] * mean_ref[q_head]
            mean = mean * (1.0 / totals[g])
            if last:
                out_ref[:, lanes(q_head)] = mean.astype(jnp.bfloat16)
            else:
                outs[0][q_head] = mean
                level = tops[g] + jnp.log2(totals[g]) * (1.0 / EXP2_SCALE)
                outs[1][q_head] = jnp.broadcast_to(level, (rows, HEAD_WIDTH))
        if last:
            done = slice(head * group * HEAD_WIDTH, (head + 1) * group * HEAD_WIDTH)
            stores.append(
                pltpu.make_async_copy(out_ref.at[:, done], out_hbm.at[:, done], sems.at[head])
            )
            stores[-1].start()

    weighed = []
    for head in range(KEY_VALUE_HEADS):
        weighed.append(weigh(head))
        if head + 2 < KEY_VALUE_HEADS:
            raws.append(raw_scores(head + 2))
        if head > 0:
            mix(head - 1, *weighed[head - 1])
    mix(KEY_VALUE_HEADS - 1, *weighed[-1])
    if last:
        for store in stores:
            store.wait()


def gathered(queries, keys, values, doc_lengths, loader_pos):
    shards = lax.axis_size("ctx")
    rows = queries.shape[0]
    heads = queries.shape[1] // HEAD_WIDTH
    vmem, smem = pl.BlockSpec(memory_space=pltpu.VMEM), pl.BlockSpec(memory_space=pltpu.SMEM)
    hbm = pl.BlockSpec(memory_space=pl.ANY)
    per_head = jax.ShapeDtypeStruct((heads, rows, HEAD_WIDTH), jnp.float32)

    def swap(x, distance):
        return lax.ppermute(x, "ctx", [(i, i ^ distance) for i in range(shards)])

    def fold(name, blocks, *state, last=False):
        n, first = len(blocks), not state
        out_shape = (per_head, per_head)
        if first:
            out_shape = (jax.ShapeDtypeStruct((2, rows, HEAD_WIDTH), jnp.float32), *out_shape)
        if last:
            out_shape = (jax.ShapeDtypeStruct(queries.shape, queries.dtype),)
        return pl.pallas_call(
            lambda *refs: fold_kernel(n, first, last, *refs),
            out_shape=out_shape,
            in_specs=([smem] if first else []) + [vmem] * (1 + len(state) + n),
            out_specs=(hbm if last else vmem,) * len(out_shape),
            scratch_shapes=[pltpu.VMEM((rows, n * rows), jnp.float32)]
            + last
            * [
                pltpu.VMEM(queries.shape, queries.dtype),
                pltpu.SemaphoreType.DMA((KEY_VALUE_HEADS,)),
            ],
            compiler_params=pltpu.CompilerParams(vmem_limit_bytes=32 << 20),
            name=name,
        )(*([doc_lengths] if first else []), queries, *state, *blocks)

    slabs = 2 * KEY_VALUE_HEADS
    own = pl.pallas_call(
        pack_kernel,
        out_shape=pltpu.VMEM((slabs * rows + POS_ROWS, HEAD_WIDTH), keys.dtype),
        in_specs=[hbm, hbm, hbm],
        out_specs=vmem,
        scratch_shapes=[
            pltpu.VMEM((1, rows), jnp.int32),
            pltpu.SemaphoreType.DMA((slabs + 1,)),
        ],
        name="pack",
    )(keys, values, loader_pos.reshape(1, rows))
    six = swap(own, 6)
    two = swap(own, 2)
    four = swap(six, 2)
    where, *state = fold("early", [own, six, two, swap(own, 1)])
    four = after(four, *state)
    state = fold("middle", [swap(six, 1), swap(two, 1), four], where, *state)
    return fold("last", [swap(four, 1)], where, *state, last=True)[0]


def on_device(queries, keys, values, doc_lengths, loader_pos):
    shards = lax.axis_size("ctx")
    if shards == GATHER_SHARDS:
        return gathered(queries, keys, values, doc_lengths, loader_pos)
    return routed(queries, keys, values, doc_lengths, loader_pos)


def solution(mesh):
    placed = (
        P(("grp", "ctx"), None),
        P(("grp", "ctx"), None),
        P(("grp", "ctx"), None),
        P("grp"),
        P(("grp", "ctx")),
    )
    return jax.shard_map(
        on_device, mesh=mesh, in_specs=placed, out_specs=P(("grp", "ctx"), None), check_vma=False
    )
```

```python
import jax
import jax.numpy as jnp
from jax import lax
from jax.experimental import pallas as pl
from jax.experimental.pallas import tpu as pltpu
from jax.sharding import PartitionSpec as P

KEY_VALUE_HEADS = 4
HEAD_WIDTH = 128
REACH = 2
GATHER_SHARDS = 8
POS_ROWS = 8


masked_value = -1e30
EXP2_SCALE = 1.4426950408889634 / HEAD_WIDTH**0.5


def shifted(block, axis, distance):
    devices = range(lax.axis_size(axis))
    route = [(i - distance, i) for i in devices if i - distance in devices]
    return lax.ppermute(block, axis, route)


def doc_index(positions, ends):
    return jnp.sum((positions[:, None] >= ends[None, :]).astype(jnp.int32), axis=1)


def attend(query_rows, k_win, v_win, q_pos, k_pos, ends):
    routed_rows = query_rows.shape[0]
    query_group = query_rows.shape[1] // (KEY_VALUE_HEADS * HEAD_WIDTH)
    q_doc = doc_index(q_pos, ends)
    k_doc = doc_index(k_pos, ends)
    allowed = (
        (k_pos[None, :] <= q_pos[:, None])
        & (q_doc[:, None] == k_doc[None, :])
        & (k_pos[None, :] >= 0)
    )
    query_head_rows = query_rows.reshape(routed_rows, KEY_VALUE_HEADS, query_group, HEAD_WIDTH)
    results = []
    for head_number in range(KEY_VALUE_HEADS):
        k_part = k_win[:, head_number * HEAD_WIDTH : (head_number + 1) * HEAD_WIDTH]
        v_part = v_win[:, head_number * HEAD_WIDTH : (head_number + 1) * HEAD_WIDTH]
        scores = jnp.einsum(
            "tgd,wd->gtw",
            query_head_rows[:, head_number],
            k_part,
            preferred_element_type=jnp.float32,
        ) * (1.0 / HEAD_WIDTH**0.5)
        scores = jnp.where(allowed[None], scores, masked_value)
        top = jnp.max(scores, axis=-1, keepdims=True)
        weight = jnp.exp(scores - top)
        total = jnp.sum(weight, axis=-1, keepdims=True)
        rounded = weight.astype(jnp.bfloat16)
        mixed = jnp.einsum(
            "gtw,wd->tgd", rounded, v_part, preferred_element_type=jnp.float32
        ) / jnp.transpose(total, (1, 0, 2))
        results.append(mixed.reshape(routed_rows, query_group * HEAD_WIDTH))
    return jnp.concatenate(results, axis=1).astype(jnp.bfloat16)


def routed(queries, keys, values, doc_lengths, loader_pos):
    routed_rows = queries.shape[0]
    shards = lax.axis_size("ctx")
    cap_rows = routed_rows // shards
    shard_index = lax.axis_index("ctx")
    first_row = shard_index * routed_rows
    window = (REACH + 1) * routed_rows
    order = jnp.argsort(loader_pos)
    send_q = queries[order].reshape(shards, cap_rows, -1)
    send_k = keys[order].reshape(shards, cap_rows, -1)
    send_v = values[order].reshape(shards, cap_rows, -1)
    send_pos = loader_pos[order].reshape(shards, cap_rows)
    got_q, got_k, got_v, got_pos = (
        lax.all_to_all(send_q, "ctx", split_axis=0, concat_axis=0, tiled=True),
        lax.all_to_all(send_k, "ctx", split_axis=0, concat_axis=0, tiled=True),
        lax.all_to_all(send_v, "ctx", split_axis=0, concat_axis=0, tiled=True),
        lax.all_to_all(send_pos, "ctx", split_axis=0, concat_axis=0, tiled=True),
    )
    local = (got_pos.reshape(-1) - first_row).astype(jnp.int32)
    place = jnp.argsort(local)
    own_q = got_q.reshape(routed_rows, -1)[place]
    own_k = got_k.reshape(routed_rows, -1)[place]
    own_v = got_v.reshape(routed_rows, -1)[place]
    pieces_k = []
    pieces_v = []
    for step in range(REACH, 0, -1):
        far_k, far_v = shifted((own_k, own_v), "ctx", step)
        pieces_k.append(far_k)
        pieces_v.append(far_v)
    win_k = jnp.concatenate(pieces_k + [own_k], axis=0)
    win_v = jnp.concatenate(pieces_v + [own_v], axis=0)
    ends = jnp.cumsum(doc_lengths)
    q_pos = first_row + jnp.arange(routed_rows, dtype=jnp.int32)
    k_pos = first_row - REACH * routed_rows + jnp.arange(window, dtype=jnp.int32)
    packed_out = attend(own_q, win_k, win_v, q_pos, k_pos, ends)
    outgoing = packed_out[local].reshape(shards, cap_rows, -1)
    returned = lax.all_to_all(outgoing, "ctx", split_axis=0, concat_axis=0, tiled=True).reshape(
        routed_rows, -1
    )
    return returned[jnp.argsort(order)]


def lanes(head):
    return slice(head * HEAD_WIDTH, (head + 1) * HEAD_WIDTH)


def after(x, *earlier):
    return lax.optimization_barrier((x, *earlier))[0]


def pack_kernel(k_ref, v_ref, pos_ref, out_ref, pos_vmem, sems):
    rows = k_ref.shape[0]
    copies = [pltpu.make_async_copy(pos_ref, pos_vmem, sems.at[2 * KEY_VALUE_HEADS])]
    for i, ref in enumerate((k_ref, v_ref)):
        for head in range(KEY_VALUE_HEADS):
            slab = i * KEY_VALUE_HEADS + head
            copies.append(
                pltpu.make_async_copy(
                    ref.at[:, lanes(head)], out_ref.at[slab * rows : (slab + 1) * rows, :], sems.at[slab]
                )
            )
    for copy in copies:
        copy.start()
    copies[0].wait()
    pos = pos_vmem[...]
    row = lax.broadcasted_iota(jnp.int32, (POS_ROWS, rows), 0)
    digits = jnp.where(row == 0, pos % 128, pos // 128)
    out_ref[2 * KEY_VALUE_HEADS * rows :, :] = digits.astype(jnp.float32).astype(jnp.bfloat16)
    for copy in copies[1:]:
        copy.wait()


def positions(block_ref):
    at = block_ref.shape[0] - POS_ROWS
    both = block_ref[at:, :].astype(jnp.float32)
    return both[0:1] + 128.0 * both[1:2]


def keys_of(block_refs, rows, head):
    return jnp.concatenate([r[head * rows : (head + 1) * rows, :] for r in block_refs], axis=0)


def values_of(block_refs, rows, head):
    return keys_of(block_refs, rows, KEY_VALUE_HEADS + head)


def write_bias(bias_ref, block_refs, q_pos, q_first):
    rows = bias_ref.shape[0]
    for s, ref in enumerate(block_refs):
        k_pos = positions(ref)
        allowed = (k_pos <= q_pos) & (k_pos >= q_first)
        bias_ref[:, s * rows : (s + 1) * rows] = jnp.where(allowed, 0.0, masked_value)


def stacked(ref, head, group):
    return jnp.concatenate([ref[:, lanes(head * group + g)] for g in range(group)], axis=0)


def fold_kernel(shards, first, last, *refs):
    if first:
        (doc_ref, q_ref), refs = refs[:2], refs[2:]
    else:
        (q_ref, where_ref, sum_ref, top_ref, total_ref), refs = refs[:5], refs[5:]
    block_refs, refs = refs[:shards], refs[shards:]
    if last:
        out_hbm, bias_ref, out_ref, sems = refs
        stores = []
    else:
        outs, bias_ref = refs[:-1], refs[-1]
    rows = q_ref.shape[0]
    group = q_ref.shape[1] // HEAD_WIDTH // KEY_VALUE_HEADS

    def raw_scores(head):
        return lax.dot_general(
            stacked(q_ref, head, group),
            keys_of(block_refs, rows, head),
            (((1,), (1,)), ((), ())),
            preferred_element_type=jnp.float32,
        )

    raws = [raw_scores(0), raw_scores(1)]
    if first:
        square = (rows, rows)
        diagonal = lax.broadcasted_iota(jnp.int32, square, 0) == lax.broadcasted_iota(jnp.int32, square, 1)
        q_pos = jnp.sum(jnp.where(diagonal, positions(block_refs[0]), 0.0), axis=1, keepdims=True)
        end, q_first = jnp.int32(0), jnp.zeros_like(q_pos)
        for j in range(doc_ref.shape[0]):
            end = end + doc_ref[j]
            limit = end.astype(jnp.float32)
            q_first = jnp.where(q_pos >= limit, limit, q_first)
        outs[0][0] = jnp.broadcast_to(q_pos, (rows, HEAD_WIDTH))
        outs[0][1] = jnp.broadcast_to(q_first, (rows, HEAD_WIDTH))
        outs = outs[1:]
    else:
        q_pos, q_first = where_ref[0], where_ref[1]
    write_bias(bias_ref, block_refs, q_pos, q_first)

    def weigh(head):
        weights, tops, totals, before = [], [], [], []
        for g in range(group):
            scores = raws[head][g * rows : (g + 1) * rows] + bias_ref[...]
            top = jnp.max(scores, axis=1, keepdims=True)
            if first:
                weight = jnp.exp2((scores - top) * EXP2_SCALE)
                total = jnp.sum(weight, axis=1, keepdims=True)
            else:
                old_top = top_ref[head * group + g]
                top = jnp.maximum(top, old_top)
                weight = jnp.exp2((scores - jnp.tile(top, (1, shards))) * EXP2_SCALE)
                before.append(jnp.exp2((old_top - top) * EXP2_SCALE))
                total = jnp.sum(weight, axis=1, keepdims=True)
                total = before[-1] * total_ref[head * group + g] + total
            weights.append(weight.astype(jnp.bfloat16))
            tops.append(top)
            totals.append(total)
        return jnp.concatenate(weights, axis=0), tops, totals, before

    def mix(head, weights, tops, totals, before):
        mixed = jnp.dot(weights, values_of(block_refs, rows, head), preferred_element_type=jnp.float32)
        for g in range(group):
            q_head = head * group + g
            found = mixed[g * rows : (g + 1) * rows]
            if not first:
                found = found + before[g] * sum_ref[q_head]
            if last:
                out_ref[:, lanes(q_head)] = (found * (1.0 / totals[g])).astype(jnp.bfloat16)
            else:
                outs[0][q_head] = found
                outs[1][q_head] = jnp.broadcast_to(tops[g], (rows, HEAD_WIDTH))
                outs[2][q_head] = jnp.broadcast_to(totals[g], (rows, HEAD_WIDTH))
        if last:
            done = slice(head * group * HEAD_WIDTH, (head + 1) * group * HEAD_WIDTH)
            stores.append(
                pltpu.make_async_copy(out_ref.at[:, done], out_hbm.at[:, done], sems.at[head])
            )
            stores[-1].start()

    weighed = []
    for head in range(KEY_VALUE_HEADS):
        weighed.append(weigh(head))
        if head + 2 < KEY_VALUE_HEADS:
            raws.append(raw_scores(head + 2))
        if head > 0:
            mix(head - 1, *weighed[head - 1])
    mix(KEY_VALUE_HEADS - 1, *weighed[-1])
    if last:
        for store in stores:
            store.wait()


def gathered(queries, keys, values, doc_lengths, loader_pos):
    shards = lax.axis_size("ctx")
    rows = queries.shape[0]
    heads = queries.shape[1] // HEAD_WIDTH
    vmem, smem = pl.BlockSpec(memory_space=pltpu.VMEM), pl.BlockSpec(memory_space=pltpu.SMEM)
    hbm = pl.BlockSpec(memory_space=pl.ANY)
    per_head = jax.ShapeDtypeStruct((heads, rows, HEAD_WIDTH), jnp.float32)

    def swap(x, distance):
        return lax.ppermute(x, "ctx", [(i, i ^ distance) for i in range(shards)])

    def fold(name, blocks, *state, last=False):
        n, first = len(blocks), not state
        out_shape = (per_head, per_head, per_head)
        if first:
            out_shape = (jax.ShapeDtypeStruct((2, rows, HEAD_WIDTH), jnp.float32), *out_shape)
        if last:
            out_shape = (jax.ShapeDtypeStruct(queries.shape, queries.dtype),)
        return pl.pallas_call(
            lambda *refs: fold_kernel(n, first, last, *refs),
            out_shape=out_shape,
            in_specs=([smem] if first else []) + [vmem] * (1 + len(state) + n),
            out_specs=(hbm if last else vmem,) * len(out_shape),
            scratch_shapes=[pltpu.VMEM((rows, n * rows), jnp.float32)]
            + last
            * [
                pltpu.VMEM(queries.shape, queries.dtype),
                pltpu.SemaphoreType.DMA((KEY_VALUE_HEADS,)),
            ],
            compiler_params=pltpu.CompilerParams(vmem_limit_bytes=32 << 20),
            name=name,
        )(*([doc_lengths] if first else []), queries, *state, *blocks)

    slabs = 2 * KEY_VALUE_HEADS
    own = pl.pallas_call(
        pack_kernel,
        out_shape=pltpu.VMEM((slabs * rows + POS_ROWS, HEAD_WIDTH), keys.dtype),
        in_specs=[hbm, hbm, hbm],
        out_specs=vmem,
        scratch_shapes=[
            pltpu.VMEM((1, rows), jnp.int32),
            pltpu.SemaphoreType.DMA((slabs + 1,)),
        ],
        name="pack",
    )(keys, values, loader_pos.reshape(1, rows))
    six = swap(own, 6)
    two = swap(own, 2)
    four = swap(six, 2)
    where, *state = fold("early", [own, six, two, swap(own, 1)])
    four = after(four, *state)
    state = fold("middle", [swap(six, 1), swap(two, 1), four], where, *state)
    return fold("last", [swap(four, 1)], where, *state, last=True)[0]


def on_device(queries, keys, values, doc_lengths, loader_pos):
    shards = lax.axis_size("ctx")
    if shards == GATHER_SHARDS:
        return gathered(queries, keys, values, doc_lengths, loader_pos)
    return routed(queries, keys, values, doc_lengths, loader_pos)


def solution(mesh):
    placed = (
        P(("grp", "ctx"), None),
        P(("grp", "ctx"), None),
        P(("grp", "ctx"), None),
        P("grp"),
        P(("grp", "ctx")),
    )
    return jax.shard_map(
        on_device, mesh=mesh, in_specs=placed, out_specs=P(("grp", "ctx"), None), check_vma=False
    )
```

```python
import jax
import jax.numpy as jnp
from jax import lax
from jax.experimental import pallas as pl
from jax.experimental.pallas import tpu as pltpu
from jax.sharding import PartitionSpec as P

KEY_VALUE_HEADS = 4
HEAD_WIDTH = 128
REACH = 2
GATHER_SHARDS = 8
POS_ROWS = 8


masked_value = -1e30
EXP2_SCALE = 1.4426950408889634 / HEAD_WIDTH**0.5


def shifted(block, axis, distance):
    devices = range(lax.axis_size(axis))
    route = [(i - distance, i) for i in devices if i - distance in devices]
    return lax.ppermute(block, axis, route)


def doc_index(positions, ends):
    return jnp.sum((positions[:, None] >= ends[None, :]).astype(jnp.int32), axis=1)


def attend(query_rows, k_win, v_win, q_pos, k_pos, ends):
    routed_rows = query_rows.shape[0]
    query_group = query_rows.shape[1] // (KEY_VALUE_HEADS * HEAD_WIDTH)
    q_doc = doc_index(q_pos, ends)
    k_doc = doc_index(k_pos, ends)
    allowed = (
        (k_pos[None, :] <= q_pos[:, None])
        & (q_doc[:, None] == k_doc[None, :])
        & (k_pos[None, :] >= 0)
    )
    query_head_rows = query_rows.reshape(routed_rows, KEY_VALUE_HEADS, query_group, HEAD_WIDTH)
    results = []
    for head_number in range(KEY_VALUE_HEADS):
        k_part = k_win[:, head_number * HEAD_WIDTH : (head_number + 1) * HEAD_WIDTH]
        v_part = v_win[:, head_number * HEAD_WIDTH : (head_number + 1) * HEAD_WIDTH]
        scores = jnp.einsum(
            "tgd,wd->gtw",
            query_head_rows[:, head_number],
            k_part,
            preferred_element_type=jnp.float32,
        ) * (1.0 / HEAD_WIDTH**0.5)
        scores = jnp.where(allowed[None], scores, masked_value)
        top = jnp.max(scores, axis=-1, keepdims=True)
        weight = jnp.exp(scores - top)
        total = jnp.sum(weight, axis=-1, keepdims=True)
        rounded = weight.astype(jnp.bfloat16)
        mixed = jnp.einsum(
            "gtw,wd->tgd", rounded, v_part, preferred_element_type=jnp.float32
        ) / jnp.transpose(total, (1, 0, 2))
        results.append(mixed.reshape(routed_rows, query_group * HEAD_WIDTH))
    return jnp.concatenate(results, axis=1).astype(jnp.bfloat16)


def routed(queries, keys, values, doc_lengths, loader_pos):
    routed_rows = queries.shape[0]
    shards = lax.axis_size("ctx")
    cap_rows = routed_rows // shards
    shard_index = lax.axis_index("ctx")
    first_row = shard_index * routed_rows
    window = (REACH + 1) * routed_rows
    order = jnp.argsort(loader_pos)
    send_q = queries[order].reshape(shards, cap_rows, -1)
    send_k = keys[order].reshape(shards, cap_rows, -1)
    send_v = values[order].reshape(shards, cap_rows, -1)
    send_pos = loader_pos[order].reshape(shards, cap_rows)
    got_q, got_k, got_v, got_pos = (
        lax.all_to_all(send_q, "ctx", split_axis=0, concat_axis=0, tiled=True),
        lax.all_to_all(send_k, "ctx", split_axis=0, concat_axis=0, tiled=True),
        lax.all_to_all(send_v, "ctx", split_axis=0, concat_axis=0, tiled=True),
        lax.all_to_all(send_pos, "ctx", split_axis=0, concat_axis=0, tiled=True),
    )
    local = (got_pos.reshape(-1) - first_row).astype(jnp.int32)
    place = jnp.argsort(local)
    own_q = got_q.reshape(routed_rows, -1)[place]
    own_k = got_k.reshape(routed_rows, -1)[place]
    own_v = got_v.reshape(routed_rows, -1)[place]
    pieces_k = []
    pieces_v = []
    for step in range(REACH, 0, -1):
        far_k, far_v = shifted((own_k, own_v), "ctx", step)
        pieces_k.append(far_k)
        pieces_v.append(far_v)
    win_k = jnp.concatenate(pieces_k + [own_k], axis=0)
    win_v = jnp.concatenate(pieces_v + [own_v], axis=0)
    ends = jnp.cumsum(doc_lengths)
    q_pos = first_row + jnp.arange(routed_rows, dtype=jnp.int32)
    k_pos = first_row - REACH * routed_rows + jnp.arange(window, dtype=jnp.int32)
    packed_out = attend(own_q, win_k, win_v, q_pos, k_pos, ends)
    outgoing = packed_out[local].reshape(shards, cap_rows, -1)
    returned = lax.all_to_all(outgoing, "ctx", split_axis=0, concat_axis=0, tiled=True).reshape(
        routed_rows, -1
    )
    return returned[jnp.argsort(order)]


def lanes(head):
    return slice(head * HEAD_WIDTH, (head + 1) * HEAD_WIDTH)


def after(x, *earlier):
    return lax.optimization_barrier((x, *earlier))[0]


def pack_kernel(k_ref, v_ref, pos_ref, out_ref, pos_vmem, sems):
    rows = k_ref.shape[0]
    copies = [pltpu.make_async_copy(pos_ref, pos_vmem, sems.at[2 * KEY_VALUE_HEADS])]
    for i, ref in enumerate((k_ref, v_ref)):
        for head in range(KEY_VALUE_HEADS):
            slab = i * KEY_VALUE_HEADS + head
            copies.append(
                pltpu.make_async_copy(
                    ref.at[:, lanes(head)], out_ref.at[slab * rows : (slab + 1) * rows, :], sems.at[slab]
                )
            )
    for copy in copies:
        copy.start()
    copies[0].wait()
    pos = pos_vmem[...]
    row = lax.broadcasted_iota(jnp.int32, (POS_ROWS, rows), 0)
    digits = jnp.where(row == 0, pos % 128, pos // 128)
    out_ref[2 * KEY_VALUE_HEADS * rows :, :] = digits.astype(jnp.float32).astype(jnp.bfloat16)
    for copy in copies[1:]:
        copy.wait()


def positions(block_ref):
    at = block_ref.shape[0] - POS_ROWS
    both = block_ref[at:, :].astype(jnp.float32)
    return both[0:1] + 128.0 * both[1:2]


def keys_of(block_refs, rows, head):
    return jnp.concatenate([r[head * rows : (head + 1) * rows, :] for r in block_refs], axis=0)


def values_of(block_refs, rows, head):
    return keys_of(block_refs, rows, KEY_VALUE_HEADS + head)


def write_bias(bias_ref, block_refs, q_pos, q_first):
    rows = bias_ref.shape[0]
    for s, ref in enumerate(block_refs):
        k_pos = positions(ref)
        allowed = (k_pos <= q_pos) & (k_pos >= q_first)
        bias_ref[:, s * rows : (s + 1) * rows] = jnp.where(allowed, 0.0, masked_value)


def stacked(ref, head, group):
    return jnp.concatenate([ref[:, lanes(head * group + g)] for g in range(group)], axis=0)


def lane_sums(weight):
    return sum(weight[:, lanes(i)] for i in range(weight.shape[1] // HEAD_WIDTH))


def fold_kernel(shards, first, last, *refs):
    if first:
        (doc_ref, q_ref), refs = refs[:2], refs[2:]
    else:
        (q_ref, where_ref, sum_ref, top_ref, total_ref), refs = refs[:5], refs[5:]
    block_refs, refs = refs[:shards], refs[shards:]
    if last:
        out_hbm, bias_ref, out_ref, sems = refs
        stores = []
    else:
        outs, bias_ref = refs[:-1], refs[-1]
    rows = q_ref.shape[0]
    group = q_ref.shape[1] // HEAD_WIDTH // KEY_VALUE_HEADS

    def raw_scores(head):
        return lax.dot_general(
            stacked(q_ref, head, group),
            keys_of(block_refs, rows, head),
            (((1,), (1,)), ((), ())),
            preferred_element_type=jnp.float32,
        )

    raws = [raw_scores(0), raw_scores(1)]
    if first:
        square = (rows, rows)
        diagonal = lax.broadcasted_iota(jnp.int32, square, 0) == lax.broadcasted_iota(jnp.int32, square, 1)
        q_pos = jnp.sum(jnp.where(diagonal, positions(block_refs[0]), 0.0), axis=1, keepdims=True)
        end, q_first = jnp.int32(0), jnp.zeros_like(q_pos)
        for j in range(doc_ref.shape[0]):
            end = end + doc_ref[j]
            limit = end.astype(jnp.float32)
            q_first = jnp.where(q_pos >= limit, limit, q_first)
        outs[0][0] = jnp.broadcast_to(q_pos, (rows, HEAD_WIDTH))
        outs[0][1] = jnp.broadcast_to(q_first, (rows, HEAD_WIDTH))
        outs = outs[1:]
    else:
        q_pos, q_first = where_ref[0], where_ref[1]
    write_bias(bias_ref, block_refs, q_pos, q_first)

    def weigh(head):
        weights, tops, totals, before = [], [], [], []
        for g in range(group):
            scores = raws[head][g * rows : (g + 1) * rows] + bias_ref[...]
            top = jnp.max(scores, axis=1, keepdims=True)
            if first:
                weight = jnp.exp2((scores - top) * EXP2_SCALE)
                total = lane_sums(weight)
            else:
                old_top = top_ref[head * group + g]
                top = jnp.maximum(top, old_top)
                weight = jnp.exp2((scores - jnp.tile(top, (1, shards))) * EXP2_SCALE)
                before.append(jnp.exp2((old_top - top) * EXP2_SCALE))
                total = before[-1] * total_ref[head * group + g] + lane_sums(weight)
                if last:
                    total = jnp.sum(total, axis=1, keepdims=True)
            weights.append(weight.astype(jnp.bfloat16))
            tops.append(top)
            totals.append(total)
        return jnp.concatenate(weights, axis=0), tops, totals, before

    def mix(head, weights, tops, totals, before):
        mixed = jnp.dot(weights, values_of(block_refs, rows, head), preferred_element_type=jnp.float32)
        for g in range(group):
            q_head = head * group + g
            found = mixed[g * rows : (g + 1) * rows]
            if not first:
                found = found + before[g] * sum_ref[q_head]
            if last:
                out_ref[:, lanes(q_head)] = (found * (1.0 / totals[g])).astype(jnp.bfloat16)
            else:
                outs[0][q_head] = found
                outs[1][q_head] = jnp.broadcast_to(tops[g], (rows, HEAD_WIDTH))
                outs[2][q_head] = totals[g]
        if last:
            done = slice(head * group * HEAD_WIDTH, (head + 1) * group * HEAD_WIDTH)
            stores.append(
                pltpu.make_async_copy(out_ref.at[:, done], out_hbm.at[:, done], sems.at[head])
            )
            stores[-1].start()

    weighed = []
    for head in range(KEY_VALUE_HEADS):
        weighed.append(weigh(head))
        if head + 2 < KEY_VALUE_HEADS:
            raws.append(raw_scores(head + 2))
        if head > 0:
            mix(head - 1, *weighed[head - 1])
    mix(KEY_VALUE_HEADS - 1, *weighed[-1])
    if last:
        for store in stores:
            store.wait()


def gathered(queries, keys, values, doc_lengths, loader_pos):
    shards = lax.axis_size("ctx")
    rows = queries.shape[0]
    heads = queries.shape[1] // HEAD_WIDTH
    vmem, smem = pl.BlockSpec(memory_space=pltpu.VMEM), pl.BlockSpec(memory_space=pltpu.SMEM)
    hbm = pl.BlockSpec(memory_space=pl.ANY)
    per_head = jax.ShapeDtypeStruct((heads, rows, HEAD_WIDTH), jnp.float32)

    def swap(x, distance):
        return lax.ppermute(x, "ctx", [(i, i ^ distance) for i in range(shards)])

    def fold(name, blocks, *state, last=False):
        n, first = len(blocks), not state
        out_shape = (per_head, per_head, per_head)
        if first:
            out_shape = (jax.ShapeDtypeStruct((2, rows, HEAD_WIDTH), jnp.float32), *out_shape)
        if last:
            out_shape = (jax.ShapeDtypeStruct(queries.shape, queries.dtype),)
        return pl.pallas_call(
            lambda *refs: fold_kernel(n, first, last, *refs),
            out_shape=out_shape,
            in_specs=([smem] if first else []) + [vmem] * (1 + len(state) + n),
            out_specs=(hbm if last else vmem,) * len(out_shape),
            scratch_shapes=[pltpu.VMEM((rows, n * rows), jnp.float32)]
            + last
            * [
                pltpu.VMEM(queries.shape, queries.dtype),
                pltpu.SemaphoreType.DMA((KEY_VALUE_HEADS,)),
            ],
            compiler_params=pltpu.CompilerParams(vmem_limit_bytes=32 << 20),
            name=name,
        )(*([doc_lengths] if first else []), queries, *state, *blocks)

    slabs = 2 * KEY_VALUE_HEADS
    own = pl.pallas_call(
        pack_kernel,
        out_shape=pltpu.VMEM((slabs * rows + POS_ROWS, HEAD_WIDTH), keys.dtype),
        in_specs=[hbm, hbm, hbm],
        out_specs=vmem,
        scratch_shapes=[
            pltpu.VMEM((1, rows), jnp.int32),
            pltpu.SemaphoreType.DMA((slabs + 1,)),
        ],
        name="pack",
    )(keys, values, loader_pos.reshape(1, rows))
    six = swap(own, 6)
    two = swap(own, 2)
    four = swap(six, 2)
    where, *state = fold("early", [own, six, two, swap(own, 1)])
    four = after(four, *state)
    state = fold("middle", [swap(six, 1), swap(two, 1), four], where, *state)
    return fold("last", [swap(four, 1)], where, *state, last=True)[0]


def on_device(queries, keys, values, doc_lengths, loader_pos):
    shards = lax.axis_size("ctx")
    if shards == GATHER_SHARDS:
        return gathered(queries, keys, values, doc_lengths, loader_pos)
    return routed(queries, keys, values, doc_lengths, loader_pos)


def solution(mesh):
    placed = (
        P(("grp", "ctx"), None),
        P(("grp", "ctx"), None),
        P(("grp", "ctx"), None),
        P("grp"),
        P(("grp", "ctx")),
    )
    return jax.shard_map(
        on_device, mesh=mesh, in_specs=placed, out_specs=P(("grp", "ctx"), None), check_vma=False
    )
```
